768 devices in a mesh: grp: 8 (over y_lo, x), tile: 96 (over y_hi, z, core).
Axes of the slice: x: 4, y: 8 (y_hi: 4, y_lo: 2; y = y_hi * 2 + y_lo), z: 12, core: 2. Of those that a mesh axis runs over, the one named last changes fastest.
Arguments:
- ocean: float32 [4, 32, 32, 12288], P(None, None, 'grp', 'tile'), may hold values from -3 to 3
- tracers: bfloat16 [10, 32, 32, 12288], P(None, None, 'grp', 'tile'), may hold values from -6 to 6
- wet_blocks: int32 [8, 768], P('grp', 'tile'), may hold values 0 or 1
- surface_light: float32 [32, 12288], P('grp', 'tile'), may hold values from 0.5 to 1.5
- rates: float32 [10, 10], replicated, may hold values from -2 to 2
Outputs:
- ocean_out: float32 [4, 32, 32, 12288], P(None, None, 'grp', 'tile')
- tracer_out: bfloat16 [10, 32, 32, 12288], P(None, None, 'grp', 'tile')
- heating: float32 [32, 32, 12288], P(None, 'grp', 'tile')
The draws below stay inside these ranges and needn't reach their ends.
All inputs are finite; a program needn't handle non-finite values. No bound on the sum of `wet_blocks` on one device may be relied on, other than what follows from the above.
Results may differ from the reference program's by a relative error of at most 0.0031.
Values may be sent and summed in bfloat16 or wider, within the bound.
No kernel may reach another device: no remote copies, remote signals or barrier semaphores. Data moves between devices by JAX's collectives and lax.ppermute only.
A program may use at most 32 MiB of HBM per device.

```python
import jax
import jax.numpy as jnp
from jax import lax

NZ = 32
NTR = 10
WBY = 4
WBX = 16
NX = 12288
NY = 32


def draw_ocean(key, part):
    vel_key = jax.random.fold_in(key, 7001)
    state_key = jax.random.fold_in(key, 7002)
    shape_half = (2, NZ, NY, NX)
    velocity = jax.random.uniform(vel_key, shape_half, jnp.float32, -3.0, 3.0)
    scalars = jnp.clip(jax.random.normal(state_key, shape_half, jnp.float32), -3.0, 3.0)
    return jnp.concatenate([velocity, scalars], 0).astype(jnp.float32)


def plant(array, own_key, low, top_value):
    longest = array.shape.index(max(array.shape))
    spots = []
    for shift in (0, 1):
        where = [jax.random.randint(jax.random.fold_in(own_key, axis), (), 0, length) for axis, length in enumerate(array.shape)]
        where[longest] = (where[longest] + shift) % array.shape[longest]
        spots.append(tuple(where))
    return array.at[spots[0]].set(low).at[spots[1]].set(top_value)


def shard_levels(stream_key, extent, cuts, low, high):
    loudness, own = 1.0, jax.random.fold_in(stream_key, 6)
    for position, shards_of in cuts:
        heights = jnp.exp(jax.random.uniform(jax.random.fold_in(own, position), (shards_of,), jnp.float32, low / len(cuts), high / len(cuts)))
        loudness = loudness * jnp.repeat(heights, extent[position] // shards_of).reshape([-1 if axis == position else 1 for axis in range(len(extent))])
    return loudness


def scatter_about(key, dims, scale, most, pieces=(), held_as=jnp.bfloat16):
    array = scale * jax.random.normal(key, dims, jnp.float32)
    if pieces:
        array = array * shard_levels(key, dims, pieces, -0.22, 0.18)
    return jnp.clip(array, -most, most).astype(held_as)


def setup_inputs(seed: int = 0) -> dict:
    key_of = jax.random.split(jax.random.key(seed), 6)
    return {
        "ocean": draw_ocean(jax.random.fold_in(key_of[5], 71), 0),
        "tracers": scatter_about(key_of[1], (NTR, NZ, NY, NX), 1.0, 6.0, ((2, 8), (3, 96))),
        "wet_blocks": plant((jax.random.randint(key_of[2], (NY // WBY, NX // WBX), 0, 3) < 2).astype(jnp.int32), jax.random.fold_in(key_of[2], 1), 0, 1),
        "surface_light": jnp.clip(0.5 + 1.0 * jax.random.uniform(key_of[3], (NY, NX), jnp.float32) ** shard_levels(key_of[3], (NY, NX), ((0, 8), (1, 96)), -0.2, 0.2), 0.5, 1.5),
        "rates": scatter_about(key_of[4], (NTR, NTR), NTR ** -0.5, 2.0, (), jnp.float32),
    }


time_step = 0.3
coriolis = 0.2
viscosity = 0.1
diffusion = 0.05
thermal = 0.2
haline = 0.15
gravity_red = 0.05
react_step = 0.5
water_atten = 0.3
chloro_atten = 0.2


def minmod(first, second):
    return 0.5 * (jnp.sign(first) + jnp.sign(second)) * jnp.minimum(jnp.abs(first), jnp.abs(second))


def ocean_tendency(padded):
    center = padded[:, :, 2:-2, 2:-2]
    east_side = padded[:, :, 2:-2, 3:-1]
    west_side = padded[:, :, 2:-2, 1:-3]
    north_side = padded[:, :, 3:-1, 2:-2]
    south_side = padded[:, :, 1:-3, 2:-2]
    grad_x = 0.5 * (east_side - west_side)
    grad_y = 0.5 * (north_side - south_side)
    laplace = east_side + west_side + north_side + south_side - 4.0 * center
    zonal_vel = center[0]
    merid_vel = center[1]
    advect = -(zonal_vel[None] * grad_x + merid_vel[None] * grad_y)
    press_x = gravity_red * jnp.cumsum(thermal * grad_x[2] - haline * grad_x[3], axis=0)
    press_y = gravity_red * jnp.cumsum(thermal * grad_y[2] - haline * grad_y[3], axis=0)
    zonal_rate = advect[0] + coriolis * merid_vel - press_x + viscosity * laplace[0]
    merid_rate = advect[1] - coriolis * zonal_vel - press_y + viscosity * laplace[1]
    heat_rate = advect[2] + diffusion * laplace[2]
    salt_rate = advect[3] + diffusion * laplace[3]
    return jnp.stack([zonal_rate, merid_rate, heat_rate, salt_rate], 0)


def limited_divergence(cells, speeds, axis):
    count = cells.shape[axis] - 4

    def part(source, start, length):
        return lax.slice_in_dim(source, start, start + length, axis=axis)

    face_speed = 0.5 * (part(speeds, 1, count + 1) + part(speeds, 2, count + 1))
    behind = part(cells, 0, count + 1)
    inside = part(cells, 1, count + 1)
    ahead = part(cells, 2, count + 1)
    beyond = part(cells, 3, count + 1)
    left_value = inside + 0.5 * minmod(inside - behind, ahead - inside)
    right_value = ahead - 0.5 * minmod(ahead - inside, beyond - ahead)
    flux = jnp.maximum(face_speed, 0.0) * left_value + jnp.minimum(face_speed, 0.0) * right_value
    return part(flux, 1, count) - part(flux, 0, count)


def tracer_tendency(cells, padded_ocean):
    zonal_row = padded_ocean[0:1, :, 2:-2, :]
    merid_col = padded_ocean[1:2, :, :, 2:-2]
    along_x = limited_divergence(cells[:, :, 2:-2, :], zonal_row, 3)
    along_y = limited_divergence(cells[:, :, :, 2:-2], merid_col, 2)
    return -(along_x + along_y)


def expand_mask(wet_blocks):
    blocks = wet_blocks.astype(jnp.float32)
    rows, cols = blocks.shape
    wide = jnp.broadcast_to(blocks[:, None, :, None], (rows, WBY, cols, WBX))
    return wide.reshape(rows * WBY, cols * WBX)


def finish(ocean_two, tracer_two, wet_blocks, surface_light, rates):
    wet_cells = expand_mask(wet_blocks)
    reaction = jnp.einsum("ab,bzyx->azyx", rates, tracer_two, precision=lax.Precision.HIGHEST)
    reacted = tracer_two + react_step * wet_cells * reaction
    attenuation = water_atten + chloro_atten * reacted[0] * reacted[0]
    depth_sum = jnp.cumsum(attenuation, axis=0)
    heating = wet_cells * surface_light * (jnp.exp(attenuation - depth_sum) - jnp.exp(-depth_sum))
    ocean_out = jnp.concatenate([ocean_two[:2], ocean_two[2:3] + time_step * heating[None], ocean_two[3:]], 0)
    return ocean_out, reacted.astype(jnp.bfloat16), heating


def pad_rim(field):
    return jnp.pad(field, ((0, 0), (0, 0), (2, 2), (2, 2)))


def section_rates(ocean_state, tracer_state):
    padded_ocean = pad_rim(ocean_state)
    ocean_rate = ocean_tendency(padded_ocean)
    tracer_rate = lax.map(lambda single: tracer_tendency(pad_rim(single[None]), padded_ocean)[0], tracer_state)
    return ocean_rate, tracer_rate


def reference(ocean, tracers, wet_blocks, surface_light, rates):
    start = tracers.astype(jnp.float32)
    ocean_rate, tracer_rate = section_rates(ocean, start)
    ocean_one = ocean + time_step * ocean_rate
    tracer_one = lax.optimization_barrier((start + time_step * tracer_rate).astype(jnp.bfloat16))
    tracer_mid = tracer_one.astype(jnp.float32)
    ocean_rate, tracer_rate = section_rates(ocean_one, tracer_mid)
    ocean_two = 0.5 * (ocean + ocean_one + time_step * ocean_rate)
    tracer_two = 0.5 * (start + tracer_mid + time_step * tracer_rate)
    return finish(ocean_two, tracer_two, wet_blocks, surface_light, rates)
```

```python
import functools

import jax
import jax.numpy as jnp
from jax import lax
from jax.experimental import pallas as pl
from jax.experimental.pallas import tpu as pltpu
from jax.sharding import PartitionSpec as P

LEVELS = 32
ROWS = 4
LANES = 128
BLOCKS = LEVELS // 8
GROUP = 24
COPIES = 5
TRACERS = 10

time_step = 0.3
coriolis = 0.2
viscosity = 0.1
diffusion = 0.05
thermal = 0.2
haline = 0.15
gravity_red = 0.05
react_step = 0.5
water_atten = 0.3
chloro_atten = 0.2

U, V, T, S = range(4)
FACES = {}
_count = 0
for _name, _first, _number in (
    ("up1", -2, 8),
    ("um1", -2, 8),
    ("vp1", -3, 9),
    ("vm1", -3, 9),
    ("up2", 0, 4),
    ("um2", 0, 4),
    ("vp2", -1, 5),
    ("vm2", -1, 5),
):
    FACES[_name] = (_count, _first)
    _count += _number
FACE_SLOTS = _count


def roll(x, shift, axis=1):
    return pltpu.roll(x, shift % x.shape[axis], axis)


def east(x):
    return roll(x, -1)


def west(x):
    return roll(x, 1)


def half_minmod(a, b):
    return 0.5 * jnp.maximum(jnp.minimum(a, b), jnp.minimum(jnp.maximum(a, b), 0.0))


def rows_of(block, y):
    return pl.ds(block * 8 * ROWS + y, 8, stride=ROWS)


def running_sum(x, sub):
    for step in (1, 2, 4):
        x = x + jnp.where(sub >= step, roll(x, step, 0), 0.0)
    return x


def last_row(x):
    return jnp.broadcast_to(x[7:8, :], x.shape)


def tendency(q, big, j):
    e = [east(q[f][j]) for f in range(4)]
    w = [west(q[f][j]) for f in range(4)]
    north = [q[f][j + 1] for f in range(4)]
    south = [q[f][j - 1] for f in range(4)]
    half_u, half_v = 0.5 * q[U][j], 0.5 * q[V][j]
    out = []
    for f in range(4):
        advect = half_u * (e[f] - w[f]) + half_v * (north[f] - south[f])
        lap = (e[f] + w[f]) + (north[f] + south[f]) - 4.0 * q[f][j]
        out.append((viscosity if f < 2 else diffusion) * lap - advect)
    press_x = 0.5 * (east(big[j]) - west(big[j]))
    press_y = 0.5 * (big[j + 1] - big[j - 1])
    out[U] = out[U] + coriolis * q[V][j] - press_x
    out[V] = out[V] - coriolis * q[U][j] - press_y
    return out


def ocean_steps(load, faces, carry, store, up, down, lane_mask):
    sub = lax.broadcasted_iota(jnp.int32, (8, LANES), 0)
    carry[...] = jnp.zeros_like(carry)

    def face(block, name, j, value):
        slot, first = FACES[name]
        faces[block, slot + j - first] = value

    def depth_sum(q, rows, base):
        big = {}
        for j in rows:
            b = (gravity_red * thermal) * q[T][j] - (gravity_red * haline) * q[S][j]
            big[j] = running_sum(b, sub) + carry[base + j]
            carry[base + j] = last_row(big[j])
        return big

    def body(block, _):
        q = [{}, {}, {}, {}]
        for f in (U, V):
            for j in range(-3, 7):
                q[f][j] = load(f, j, block)
        for f in (T, S):
            for j in range(-2, 6):
                q[f][j] = load(f, j, block)
        scale = 0.5 * time_step
        for j in range(-2, 6):
            speed = scale * (q[U][j] + east(q[U][j]))
            face(block, "up1", j, jnp.maximum(speed, 0.0))
            face(block, "um1", j, jnp.minimum(speed, 0.0))
        for j in range(-3, 6):
            speed = scale * (q[V][j] + q[V][j + 1])
            face(block, "vp1", j, jnp.maximum(speed, 0.0))
            face(block, "vm1", j, jnp.minimum(speed, 0.0))
        big = depth_sum(q, range(-2, 6), 2)
        one = [{}, {}, {}, {}]
        for j in range(-1, 5):
            rate = tendency(q, big, j)
            for f in range(4):
                value = q[f][j] + time_step * rate[f]
                if j < 0:
                    value = value * up
                if j > 3:
                    value = value * down
                if lane_mask is not None:
                    value = value * lane_mask
                one[f][j] = value
        for j in range(4):
            speed = scale * (one[U][j] + east(one[U][j]))
            face(block, "up2", j, jnp.maximum(speed, 0.0))
            face(block, "um2", j, jnp.minimum(speed, 0.0))
        for j in range(-1, 4):
            speed = scale * (one[V][j] + one[V][j + 1])
            face(block, "vp2", j, jnp.maximum(speed, 0.0))
            face(block, "vm2", j, jnp.minimum(speed, 0.0))
        big = depth_sum(one, range(-1, 5), 9)
        for j in range(4):
            rate = tendency(one, big, j)
            for f in range(4):
                store(f, j, block, 0.5 * (q[f][j] + one[f][j] + time_step * rate[f]))
        return 0

    lax.fori_loop(0, BLOCKS, body, 0)


def divergence(c, low, high, face):
    diff = {j: c[j + 1] - c[j] for j in range(low - 2, high + 1)}
    slope = {j: half_minmod(diff[j - 1], diff[j]) for j in range(low - 1, high + 1)}
    flux = {
        j: face("vp", j) * (c[j] + slope[j]) + face("vm", j) * (c[j + 1] - slope[j + 1])
        for j in range(low - 1, high)
    }
    out = {}
    for j in range(low, high):
        d = east(c[j]) - c[j]
        s = half_minmod(west(d), d)
        fx = face("up", j) * (c[j] + s) + face("um", j) * east(c[j] - s)
        out[j] = (fx - west(fx)) + (flux[j] - flux[j - 1])
    return out


def tracer_steps(load, faces, block, up, down, lane_mask):
    def face_of(stage):
        def get(name, j):
            slot, first = FACES[name + stage]
            return faces[block, slot + j - first]

        return get

    c = {j: load(j) for j in range(-4, 8)}
    change = divergence(c, -2, 6, face_of("1"))
    one = {}
    for j in range(-2, 6):
        value = c[j] - change[j]
        if j < 0:
            value = value * up
        if j > 3:
            value = value * down
        if lane_mask is not None:
            value = value * lane_mask
        one[j] = value.astype(jnp.bfloat16).astype(jnp.float32)
    change = divergence(one, 0, 4, face_of("2"))
    return [0.5 * (c[j] + one[j] - change[j]) for j in range(4)]


def place(j):
    return (j + 4) // 4, (j + 4) % 4


def edges_kernel(tr, tu, td, oc, ou, od, out):
    lane = lax.broadcasted_iota(jnp.int32, (LANES, LANES), 1)
    for tile, (tracer, ocean) in enumerate(((tu, ou), (tr, oc), (td, od))):
        acc = jnp.zeros((LANES, LANES), jnp.float32)
        for f in range(TRACERS + 4):
            x = tracer[f].astype(jnp.float32) if f < TRACERS else ocean[f - TRACERS]
            acc = jnp.where((lane >= 8 * f) & (lane < 8 * f + 8), roll(x, 8 * f + 4), acc)
        out[tile] = acc


def main_kernel(flags, tr, tu, td, oc, ou, od, two, ocean_two, strip, ocean_strip, faces, carry, cells):
    up, down = flags[0], flags[1]
    ocean = (ou, oc, od)

    def load(f, j, block):
        tile, y = place(j)
        return ocean[tile][f, rows_of(block, y), :]

    def store(f, j, block, value):
        ocean_two[f, j, pl.ds(block * 8, 8), :] = value

    ocean_steps(load, faces, carry, store, up, down, None)

    def body(t, _):
        for tile, ref in enumerate((tu, tr, td)):
            cells[tile] = ref[t].astype(jnp.float32)
        for block in range(BLOCKS):

            def cell(j):
                tile, y = place(j)
                return cells[tile, rows_of(block, y), :]

            result = tracer_steps(cell, faces, block, up, down, None)
            for j in range(4):
                two[t, j, block * 8 : block * 8 + 8, :] = result[j]
        return 0

    lax.fori_loop(0, TRACERS, body, 0)

    lane = lax.broadcasted_iota(jnp.int32, (LANES, LANES), 1)

    def own(x, base, acc):
        acc = jnp.where((lane >= base) & (lane < base + 8), roll(x, base + 8), acc)
        return jnp.where((lane >= base + 16) & (lane < base + 24), roll(x, base + 16), acc)

    for tile, (tracer, sea) in enumerate(((tu, ou), (tr, oc), (td, od))):
        for half in range(2):
            acc = jnp.zeros((LANES, LANES), jnp.float32)
            for k in range(COPIES):
                acc = own(tracer[half * COPIES + k].astype(jnp.float32), GROUP * k, acc)
            strip[half, tile] = acc
        for f in range(4):
            ocean_strip[f, tile] = own(sea[f], 0, jnp.zeros((LANES, LANES), jnp.float32))


def finish_kernel(
    flags, rates, wet_blocks, light, two, ocean_two, strip, ocean_strip, from_left, from_right,
    ocean_out, tracer_out, heating, faces, carry, cells, seas, strip_two, strip_ocean, reacted,
):
    up, down, left, right = (flags[k] for k in range(4))
    lane = lax.broadcasted_iota(jnp.int32, (LANES, LANES), 1)
    for tile in range(3):
        halo = jnp.where(lane % 8 < 4, roll(from_right[tile], -4), roll(from_left[tile], 4))

        def with_halo(f, base, x):
            return jnp.where((lane >= base + 8) & (lane < base + 16), roll(halo, base + 8 - 8 * f), x)

        for half in range(2):
            acc = strip[half, tile]
            for k in range(COPIES):
                acc = with_halo(half * COPIES + k, GROUP * k, acc)
            cells[half, tile] = acc
        for f in range(4):
            one = with_halo(TRACERS + f, 0, ocean_strip[f, tile])
            pair = one + roll(one, GROUP)
            seas[f, tile] = pair + roll(pair, 2 * GROUP) + roll(one, 4 * GROUP)
    place_in = lax.broadcasted_iota(jnp.int32, (8, LANES), 1) % GROUP
    lane_mask = jnp.where((place_in >= 8) & (place_in < 12), right, jnp.where((place_in >= 12) & (place_in < 16), left, 1.0))

    def load(f, j, block):
        tile, y = place(j)
        return seas[f, tile, rows_of(block, y), :]

    def store(f, j, block, value):
        strip_ocean[f, j, pl.ds(block * 8, 8), :] = value

    ocean_steps(load, faces, carry, store, up, down, lane_mask)

    def body(block, _):
        for half in range(2):

            def cell(j):
                tile, y = place(j)
                return cells[half, tile, rows_of(block, y), :]

            result = tracer_steps(cell, faces, block, up, down, lane_mask)
            for j in range(4):
                strip_two[half, j, pl.ds(block * 8, 8), :] = result[j]
        return 0

    lax.fori_loop(0, BLOCKS, body, 0)
    lanes = lax.broadcasted_iota(jnp.int32, (8, LANES), 1)
    sub = lax.broadcasted_iota(jnp.int32, (8, LANES), 0)
    wet = jnp.zeros((8, LANES), jnp.float32)
    for k in range(8):
        wet = jnp.where(lanes // 16 == k, wet_blocks[0, k].astype(jnp.float32), wet)
    half_wet = react_step * wet

    def patched(x, edge, base):
        x = jnp.where(lanes >= LANES - 4, roll(edge, 120 - base), x)
        return jnp.where(lanes < 4, roll(edge, -16 - base), x)

    def last(block, sums):
        sums = list(sums)
        at = pl.ds(block * 8, 8)
        for y in range(ROWS):
            edge = [strip_two[half, y, at, :] for half in range(2)]
            c = [patched(two[t, y, at, :], edge[t // COPIES], GROUP * (t % COPIES)) for t in range(TRACERS)]
            for a in range(TRACERS):
                total = rates[a, 0] * c[0]
                for b in range(1, TRACERS):
                    total = total + rates[a, b] * c[b]
                value = c[a] + half_wet * total
                reacted[a, rows_of(block, y), :] = value
                if a == 0:
                    att = water_atten + chloro_atten * value * value
            cum = running_sum(att, sub) + sums[y]
            sums[y] = last_row(cum)
            heat = wet * light[y : y + 1, :] * (jnp.exp(att - cum) - jnp.exp(-cum))
            heating[rows_of(block, y), :] = heat
            for f in range(4):
                value = patched(ocean_two[f, y, at, :], strip_ocean[f, y, at, :], 0)
                if f == T:
                    value = value + time_step * heat
                ocean_out[f, rows_of(block, y), :] = value
        return tuple(sums)

    zero = jnp.zeros((8, LANES), jnp.float32)
    lax.fori_loop(0, BLOCKS, last, (zero,) * ROWS)
    for a in range(TRACERS):
        tracer_out[a] = reacted[a].astype(jnp.bfloat16)


def vmem(count):
    return [pl.BlockSpec(memory_space=pltpu.VMEM)] * count


def smem(count):
    return [pl.BlockSpec(memory_space=pltpu.SMEM)] * count


def f32(*shape):
    return jax.ShapeDtypeStruct(shape, jnp.float32)


def limit(mib):
    return pltpu.CompilerParams(vmem_limit_bytes=mib << 20)


def cost(flops, size):
    return pl.CostEstimate(flops=flops, bytes_accessed=size, transcendentals=0)


STEP_SCRATCH = [
    pltpu.VMEM((BLOCKS, FACE_SLOTS, 8, LANES), jnp.float32),
    pltpu.VMEM((14, 8, LANES), jnp.float32),
]


def shards(ocean, tracers, wet_blocks, surface_light, rates):
    tr = tracers.reshape(TRACERS, LANES, LANES)
    oc = ocean.reshape(4, LANES, LANES)
    groups, tiles = lax.axis_size("grp"), lax.axis_size("tile")

    def shifted(x, axis, count):
        ahead = [(i, i + 1) for i in range(count - 1)]
        return lax.ppermute(x, axis, ahead), lax.ppermute(x, axis, [(j, i) for i, j in ahead])

    tu, td = shifted(tr, "grp", groups)
    ou, od = shifted(oc, "grp", groups)
    g, t = lax.axis_index("grp"), lax.axis_index("tile")
    flags = jnp.stack([g > 0, g < groups - 1, t > 0, t < tiles - 1]).astype(jnp.float32)
    fields = (tr, tu, td, oc, ou, od)
    edges = pl.pallas_call(
        edges_kernel, out_shape=f32(3, LANES, LANES), in_specs=vmem(6), out_specs=vmem(1)[0], compiler_params=limit(16), name="edges"
    )(*fields)
    from_left, from_right = shifted(edges, "tile", tiles)
    main = pl.pallas_call(
        main_kernel,
        out_shape=(
            f32(TRACERS, ROWS, LEVELS, LANES),
            f32(4, ROWS, LEVELS, LANES),
            f32(2, 3, LANES, LANES),
            f32(4, 3, LANES, LANES),
        ),
        in_specs=smem(1) + vmem(6),
        out_specs=vmem(4),
        scratch_shapes=STEP_SCRATCH + [pltpu.VMEM((3, LANES, LANES), jnp.float32)],
        cost_estimate=cost(40_000_000, 4_000_000),
        compiler_params=limit(16),
        name="main",
    )(flags, *fields)
    ocean_out, tracer_out, heating = pl.pallas_call(
        finish_kernel,
        out_shape=(
            f32(4, LANES, LANES),
            jax.ShapeDtypeStruct((TRACERS, LANES, LANES), jnp.bfloat16),
            f32(LANES, LANES),
        ),
        in_specs=smem(3) + vmem(7),
        out_specs=vmem(3),
        scratch_shapes=STEP_SCRATCH
        + [
            pltpu.VMEM((2, 3, LANES, LANES), jnp.float32),
            pltpu.VMEM((4, 3, LANES, LANES), jnp.float32),
            pltpu.VMEM((2, ROWS, LEVELS, LANES), jnp.float32),
            pltpu.VMEM((4, ROWS, LEVELS, LANES), jnp.float32),
            pltpu.VMEM((TRACERS, LANES, LANES), jnp.float32),
        ],
        compiler_params=limit(16),
        name="finish",
    )(flags, rates, wet_blocks, surface_light, *main, from_left, from_right)
    return (
        ocean_out.reshape(ocean.shape),
        tracer_out.reshape(tracers.shape),
        heating.reshape(LEVELS, ROWS, LANES),
    )


def solution(mesh):
    return jax.shard_map(
        shards,
        mesh=mesh,
        in_specs=(
            P(None, None, "grp", "tile"),
            P(None, None, "grp", "tile"),
            P("grp", "tile"),
            P("grp", "tile"),
            P(),
        ),
        out_specs=(
            P(None, None, "grp", "tile"),
            P(None, None, "grp", "tile"),
            P(None, "grp", "tile"),
        ),
        check_vma=False,
    )
```

```python
import jax
import jax.numpy as jnp
from jax import lax
from jax.experimental import pallas as pl
from jax.experimental.pallas import tpu as pltpu
from jax.sharding import PartitionSpec as P

LEVELS = 32
ROWS = 4
LANES = 128
BLOCKS = LEVELS // 8
GROUP = 24
COPIES = 5
TRACERS = 10

time_step = 0.3
coriolis = 0.2
viscosity = 0.1
diffusion = 0.05
thermal = 0.2
haline = 0.15
gravity_red = 0.05
react_step = 0.5
water_atten = 0.3
chloro_atten = 0.2

U, V, T, S = range(4)
FACES = {}
_count = 0
for _name, _first, _number in (
    ("up1", -2, 8),
    ("um1", -2, 8),
    ("vp1", -3, 9),
    ("vm1", -3, 9),
    ("up2", 0, 4),
    ("um2", 0, 4),
    ("vp2", -1, 5),
    ("vm2", -1, 5),
):
    FACES[_name] = (_count, _first)
    _count += _number
FACE_SLOTS = _count
HALO_BEFORE = [(f, j) for f in (U, V) for j in (-3, -2, -1)] + [(f, j) for f in (T, S) for j in (-2, -1)]
HALO_AFTER = [(f, j) for f in (U, V) for j in (4, 5, 6)] + [(f, j) for f in (T, S) for j in (4, 5)]
HALO = {key: k for k, key in enumerate(HALO_BEFORE + HALO_AFTER)}
STRIP = {key: k for k, key in enumerate([(f, j) for f in (U, V) for j in range(-3, 7)] + [(f, j) for f in (T, S) for j in range(-2, 6)])}
PARTS = 2 * len(HALO_BEFORE)


def roll(x, shift, axis=1):
    return pltpu.roll(x, shift % x.shape[axis], axis)


def east(x):
    return roll(x, -1)


def west(x):
    return roll(x, 1)


def minmod(a, b):
    return jnp.maximum(jnp.minimum(a, b), jnp.minimum(jnp.maximum(a, b), 0.0))


def rows_of(block, y):
    return pl.ds(block * 8 * ROWS + y, 8, stride=ROWS)


def running_sum(x, sub):
    for step in (1, 2, 4):
        x = x + jnp.where(sub >= step, roll(x, step, 0), 0.0)
    return x


def last_row(x):
    return jnp.broadcast_to(x[7:8, :], x.shape)


def tendency(q, big, j):
    e = [east(q[f][j]) for f in range(4)]
    w = [west(q[f][j]) for f in range(4)]
    north = [q[f][j + 1] for f in range(4)]
    south = [q[f][j - 1] for f in range(4)]
    half_u, half_v = 0.5 * q[U][j], 0.5 * q[V][j]
    out = []
    for f in range(4):
        advect = half_u * (e[f] - w[f]) + half_v * (north[f] - south[f])
        lap = (e[f] + w[f]) + (north[f] + south[f]) - 4.0 * q[f][j]
        out.append((viscosity if f < 2 else diffusion) * lap - advect)
    press_x = 0.5 * (east(big[j]) - west(big[j]))
    press_y = 0.5 * (big[j + 1] - big[j - 1])
    out[U] = out[U] + coriolis * q[V][j] - press_x
    out[V] = out[V] - coriolis * q[U][j] - press_y
    return out


def ocean_steps(load, faces, carry, store, up, down, lane_mask, spread):
    sub = lax.broadcasted_iota(jnp.int32, (8, LANES), 0)
    carry[...] = jnp.zeros_like(carry)
    scale = 0.25 * time_step

    def body(block, _):
        at = pl.ds(block * 8, 8)

        def speeds(stage, axis, j, a, b):
            speed = spread(scale * (a + b))
            for sign, part in (("p", jnp.maximum), ("m", jnp.minimum)):
                slot, first = FACES[axis + sign + stage]
                faces[slot + j - first, at, :] = part(speed, 0.0)

        def depth_sum(q, rows, base):
            big = {}
            for j in rows:
                b = (gravity_red * thermal) * q[T][j] - (gravity_red * haline) * q[S][j]
                big[j] = running_sum(b, sub) + carry[base + j]
                carry[base + j] = last_row(big[j])
            return big

        q = [{}, {}, {}, {}]
        for f, j in STRIP:
            q[f][j] = load(f, j, at)
        for j in range(-2, 6):
            speeds("1", "u", j, q[U][j], east(q[U][j]))
        for j in range(-3, 6):
            speeds("1", "v", j, q[V][j], q[V][j + 1])
        big = depth_sum(q, range(-2, 6), 2)
        one = [{}, {}, {}, {}]
        for j in range(-1, 5):
            rate = tendency(q, big, j)
            for f in range(4):
                value = q[f][j] + time_step * rate[f]
                if j < 0:
                    value = value * up
                if j > 3:
                    value = value * down
                if lane_mask is not None:
                    value = value * lane_mask
                one[f][j] = value
        for j in range(4):
            speeds("2", "u", j, one[U][j], east(one[U][j]))
        for j in range(-1, 4):
            speeds("2", "v", j, one[V][j], one[V][j + 1])
        big = depth_sum(one, range(-1, 5), 9)
        for j in range(4):
            rate = tendency(one, big, j)
            for f in range(4):
                store(f, j, at, 0.5 * (q[f][j] + one[f][j] + time_step * rate[f]))
        return 0

    lax.fori_loop(0, BLOCKS, body, 0)


def advance(c, low, high, face, finish):
    diff_before = c(low - 1) - c(low - 2)
    left_before = flux_before = None
    for j in range(low - 1, high + 1):
        here = c(j)
        diff = c(j + 1) - here
        slope = minmod(diff_before, diff)
        twice = here + here
        flux = None
        if left_before is not None:
            flux = face("vp", j - 1) * left_before + face("vm", j - 1) * (twice - slope)
        if flux_before is not None:
            cell = c(j - 1)
            plus, minus, further = east(cell), west(cell), roll(cell, -2)
            d = plus - cell
            s = minmod(cell - minus, d)
            right = (plus + plus) - minmod(d, further - plus)
            fx = face("up", j - 1) * ((cell + cell) + s) + face("um", j - 1) * right
            finish(j - 1, (fx - west(fx)) + (flux - flux_before))
        diff_before, left_before, flux_before = diff, twice + slope, flux


def tracer_steps(load, faces, at, up, down, lane_mask, store):
    def face_of(stage):
        def get(name, j):
            slot, first = FACES[name + stage]
            return faces[slot + j - first, at, :]

        return get

    cells, one = {}, {}

    def cell(j):
        if j not in cells:
            cells[j] = load(j)
        return cells[j]

    def first(j, change):
        value = cell(j) - change
        if j == -1:
            value = value * up
        if j == ROWS:
            value = value * down
        if lane_mask is not None:
            value = value * lane_mask
        one[j] = value.astype(jnp.bfloat16).astype(jnp.float32)

    def second(j, change):
        store(j, 0.5 * ((cell(j) + one[j]) - change))

    advance(cell, -2, ROWS + 2, face_of("1"), first)
    advance(lambda j: one[j], 0, ROWS, face_of("2"), second)


def whole_iota(axis):
    return lax.broadcasted_iota(jnp.int32, (LANES, LANES), axis)


def one_hot(where):
    return jnp.where(where, 1.0, 0.0).astype(jnp.bfloat16)


def level_rows(y):
    return slice(y * LEVELS, (y + 1) * LEVELS)


def pack_kernel(tr, oc, to_next, to_previous, own_ocean, edges, tracer_in, ocean_in, sems):
    half = pl.ds(0, COPIES), pl.ds(COPIES, COPIES)
    copies = [pltpu.make_async_copy(tr.at[half[k]], tracer_in.at[half[k]], sems.at[k]) for k in range(2)]
    copies.append(pltpu.make_async_copy(oc, ocean_in, sems.at[2]))
    for copy in copies:
        copy.start()
    row, lane = whole_iota(0), whole_iota(1)
    reorder = one_hot(lane == (row % LEVELS) * ROWS + row // LEVELS)
    acc = jnp.zeros((LANES, LANES), jnp.float32)

    def with_edges(acc, x, base):
        acc = jnp.where((lane >= base) & (lane < base + 4), roll(x, base), acc)
        return jnp.where((lane >= base + 4) & (lane < base + 8), roll(x, base + 8), acc)

    for k in range(TRACERS):
        if k % COPIES == 0:
            copies[k // COPIES].wait()
        x = jnp.dot(reorder, tracer_in[k], preferred_element_type=jnp.float32)
        narrow = x.astype(jnp.bfloat16)
        to_next[k * LANES : (k + 1) * LANES, :] = narrow
        to_previous[k * LANES : (k + 1) * LANES, :] = narrow
        acc = with_edges(acc, x, GROUP * (k % COPIES) + 8 + 8 * (k // COPIES))
    base = TRACERS * LANES
    copies[2].wait()
    for f in range(4):
        levels = []
        for y in range(ROWS):
            x = ocean_in[f, pl.ds(y, LEVELS, stride=ROWS), :]
            own_ocean[f, level_rows(y), :] = x
            high = x.astype(jnp.bfloat16)
            low = (x - high.astype(jnp.float32)).astype(jnp.bfloat16)
            levels.append((high, low))
        acc = with_edges(acc, own_ocean[f], GROUP * f)
        wanted = ((1, 2, 3), (0, 1, 2)) if f in (U, V) else ((2, 3), (0, 1))
        parts = [[part for y in rows for part in levels[y]] for rows in wanted]
        for out, side in zip((to_next, to_previous), parts):
            for k, part in enumerate(side):
                out[base + k * LEVELS : base + (k + 1) * LEVELS, :] = part
        base += len(parts[0]) * LEVELS
    edges[...] = acc


def main_kernel(flags, mine, before, after, own_ocean, two, ocean_two, strip, ocean_strip, faces, carry, halo):
    up, down = flags[0], flags[1]
    sides = (before, mine, after)
    for side, names in ((before, HALO_BEFORE), (after, HALO_AFTER)):

        def part(k):
            at = TRACERS * LANES + k * LEVELS
            return side[at : at + LEVELS, :].astype(jnp.float32)

        for k, key in enumerate(names):
            halo[HALO[key]] = part(2 * k) + part(2 * k + 1)

    def load(f, j, at):
        if 0 <= j < ROWS:
            return own_ocean[f, pl.ds(at.start + j * LEVELS, 8), :]
        return halo[HALO[f, j], at, :]

    def store(f, j, at, value):
        ocean_two[f, j, at, :] = value

    ocean_steps(load, faces, carry, store, up, down, None, lambda x: x)

    def body(t, _):
        for part in range(LEVELS // 16):
            for half in range(2):

                def cell(j):
                    y = (j + 4) % 4
                    at = pl.multiple_of(t * LANES + y * LEVELS + part * 16, 16)
                    return sides[(j + 4) // 4][pl.ds(at, 16), :].astype(jnp.float32)[half * 8 : half * 8 + 8]

                at = slice(part * 16 + half * 8, part * 16 + half * 8 + 8)

                def put(j, value):
                    two[t, j, at, :] = value

                tracer_steps(cell, faces, at, up, down, None, put)
        return 0

    lax.fori_loop(0, TRACERS, body, 0)

    row, lane = whole_iota(0), whole_iota(1)
    source = jnp.where(row >= LANES - 8, row - (LANES - 8), jnp.where(row < 8, row + 16, -LANES * 4))
    picks = [one_hot(lane == source + GROUP * k) for k in range(COPIES)]
    for tile in range(3):
        for half in range(2):
            acc = None
            for k in range(COPIES):
                at = (half * COPIES + k) * LANES
                term = jnp.dot(sides[tile][at : at + LANES, :], picks[k], preferred_element_type=jnp.float32)
                acc = term if acc is None else acc + term
            strip[half, tile] = acc
    lanes = lax.broadcasted_iota(jnp.int32, (LEVELS, LANES), 1)
    for (f, j), k in STRIP.items():
        x = own_ocean[f, level_rows(j), :] if 0 <= j < ROWS else halo[HALO[f, j]]
        x = jnp.where(lanes < 8, roll(x, 8), roll(x, 16))
        ocean_strip[k] = jnp.where((lanes < 8) | ((lanes >= 16) & (lanes < 24)), x, 0.0)


def finish_kernel(
    flags, two, ocean_two, strip, ocean_strip, halo, halo_before, halo_after, rates_in, wet_in, light_in,
    ocean_out, tracer_out, heating, faces, carry, cells, strip_two, strip_ocean, reacted, narrow, ocean_done, heat_done,
    rates, wet_blocks, light, sems,
):
    small = [
        pltpu.make_async_copy(source, target, sems.at[k])
        for k, (source, target) in enumerate(((rates_in, rates), (wet_in, wet_blocks), (light_in, light)))
    ]
    for copy in small:
        copy.start()
    up, down, left, right = (flags[k] for k in range(4))
    lanes = lax.broadcasted_iota(jnp.int32, (LEVELS, LANES), 1)

    def halo_row(j):
        if j < 0:
            return halo_before[level_rows(j + 2), :]
        if j < ROWS:
            return halo[level_rows(j), :]
        return halo_after[level_rows(j - ROWS), :]

    middle = (lanes % GROUP >= 8) & (lanes % GROUP < 16)
    for j in range(-4, 8):
        tile, y = (j + 4) // 4, (j + 4) % 4
        for half in range(2):
            x = strip[half, tile, level_rows(y), :]
            if -2 <= j < 6:
                fresh = halo_row(j)
                x = jnp.where(middle, roll(fresh, -8) if half else fresh, x)
            cells[half, j + 4] = x

    place_in = lax.broadcasted_iota(jnp.int32, (8, LANES), 1)
    first_group = place_in < GROUP
    first_middle = (place_in >= 8) & (place_in < 16)
    place_in = place_in % GROUP
    lane_mask = jnp.where((place_in >= 8) & (place_in < 12), right, jnp.where((place_in >= 12) & (place_in < 16), left, 1.0))

    def load(f, j, at):
        x = ocean_strip[STRIP[f, j], at, :]
        if -2 <= j < 6:
            if j < 0:
                fresh = halo_before[pl.ds(at.start + (j + 2) * LEVELS, 8), :]
            elif j < ROWS:
                fresh = halo[pl.ds(at.start + j * LEVELS, 8), :]
            else:
                fresh = halo_after[pl.ds(at.start + (j - ROWS) * LEVELS, 8), :]
            x = jnp.where(first_middle, roll(fresh, 8 - GROUP * f), x)
        return x

    def store(f, j, at, value):
        strip_ocean[f, j, at, :] = value

    def spread(x):
        x = jnp.where(first_group, x, 0.0)
        pair = x + roll(x, GROUP)
        return pair + roll(pair, 2 * GROUP) + roll(x, 4 * GROUP)

    ocean_steps(load, faces, carry, store, up, down, lane_mask, spread)

    def body(block, _):
        at = pl.ds(block * 8, 8)
        for half in range(2):

            def put(j, value):
                strip_two[half, j, at, :] = value

            tracer_steps(lambda j: cells[half, j + 4, at, :], faces, at, up, down, lane_mask, put)
        return 0

    lax.fori_loop(0, BLOCKS, body, 0)
    for copy in small:
        copy.wait()
    lane = lax.broadcasted_iota(jnp.int32, (8, LANES), 1)
    sub = lax.broadcasted_iota(jnp.int32, (8, LANES), 0)
    wet = jnp.zeros((8, LANES), jnp.float32)
    for k in range(8):
        wet = jnp.where(lane // 16 == k, wet_blocks[0, k].astype(jnp.float32), wet)
    half_wet = react_step * wet

    def patched(x, edge, base):
        x = jnp.where(lane >= LANES - 4, roll(edge, 120 - base), x)
        return jnp.where(lane < 4, roll(edge, -16 - base), x)

    def results(block):
        rows = pl.ds(pl.multiple_of(block * 8 * ROWS, 8 * ROWS), 8 * ROWS)
        return (
            pltpu.make_async_copy(narrow.at[:, rows, :], tracer_out.at[:, rows, :], sems.at[3 + block]),
            pltpu.make_async_copy(ocean_done.at[:, rows, :], ocean_out.at[:, rows, :], sems.at[3 + BLOCKS + block]),
            pltpu.make_async_copy(heat_done.at[rows, :], heating.at[rows, :], sems.at[3 + 2 * BLOCKS + block]),
        )

    def last(block, sums):
        sums = list(sums)
        at = pl.ds(block * 8, 8)
        for pair in range(0, ROWS, 2):
            ys = (pair, pair + 1)
            edge = {y: [strip_two[half, y, at, :] for half in range(2)] for y in ys}
            c = {
                y: [patched(two[t, y, at, :], edge[y][t // COPIES], GROUP * (t % COPIES)) for t in range(TRACERS)]
                for y in ys
            }
            att = {}
            for a in range(TRACERS):
                total = {}
                for b in range(TRACERS):
                    rate = rates[a, b]
                    for y in ys:
                        term = rate * c[y][b]
                        total[y] = term if b == 0 else total[y] + term
                for y in ys:
                    value = c[y][a] + half_wet * total[y]
                    reacted[a, rows_of(block, y), :] = value
                    if a == 0:
                        att[y] = water_atten + chloro_atten * value * value
            for y in ys:
                cum = running_sum(att[y], sub) + sums[y]
                sums[y] = last_row(cum)
                heat = wet * light[y : y + 1, :] * (jnp.exp(att[y] - cum) - jnp.exp(-cum))
                heat_done[rows_of(block, y), :] = heat
                for f in range(4):
                    value = patched(ocean_two[f, y, at, :], strip_ocean[f, y, at, :], 0)
                    if f == T:
                        value = value + time_step * heat
                    ocean_done[f, rows_of(block, y), :] = value
        rows = pl.ds(pl.multiple_of(block * 8 * ROWS, 8 * ROWS), 8 * ROWS)
        narrow[:, rows, :] = reacted[:, rows, :].astype(jnp.bfloat16)
        for copy in results(block):
            copy.start()
        return tuple(sums)

    zero = jnp.zeros((8, LANES), jnp.float32)
    lax.fori_loop(0, BLOCKS, last, (zero,) * ROWS)
    for block in range(BLOCKS):
        for copy in results(block):
            copy.wait()


def vmem(count):
    return [pl.BlockSpec(memory_space=pltpu.VMEM)] * count


def smem(count):
    return [pl.BlockSpec(memory_space=pltpu.SMEM)] * count


def hbm(count):
    return [pl.BlockSpec(memory_space=pltpu.HBM)] * count


def in_hbm(x):
    return pltpu.with_memory_space_constraint(x, pltpu.HBM)


def f32(*shape):
    return jax.ShapeDtypeStruct(shape, jnp.float32)


def bf16(*shape):
    return jax.ShapeDtypeStruct(shape, jnp.bfloat16)


def limit(mib):
    return pltpu.CompilerParams(vmem_limit_bytes=mib << 20)


def cost(flops, size):
    return pl.CostEstimate(flops=flops, bytes_accessed=size, transcendentals=0)


STEP_SCRATCH = [
    pltpu.VMEM((FACE_SLOTS, LEVELS, LANES), jnp.float32),
    pltpu.VMEM((14, 8, LANES), jnp.float32),
]


def pack(tr, oc):
    payload = TRACERS * LANES + PARTS * LEVELS
    return pl.pallas_call(
        pack_kernel,
        out_shape=(bf16(payload, LANES), bf16(payload, LANES), f32(4, LANES, LANES), f32(LANES, LANES)),
        in_specs=hbm(2),
        out_specs=vmem(4),
        scratch_shapes=[
            pltpu.VMEM((TRACERS, LANES, LANES), jnp.bfloat16),
            pltpu.VMEM((4, LANES, LANES), jnp.float32),
            pltpu.SemaphoreType.DMA((3,)),
        ],
        compiler_params=limit(8),
        name="pack",
    )(in_hbm(tr), in_hbm(oc))


def transport(flags, mine, before, after, own_ocean):
    return pl.pallas_call(
        main_kernel,
        out_shape=(
            f32(TRACERS, ROWS, LEVELS, LANES),
            f32(4, ROWS, LEVELS, LANES),
            f32(2, 3, LANES, LANES),
            f32(len(STRIP), LEVELS, LANES),
        ),
        in_specs=smem(1) + vmem(4),
        out_specs=vmem(4),
        scratch_shapes=STEP_SCRATCH + [pltpu.VMEM((len(HALO), LEVELS, LANES), jnp.float32)],
        cost_estimate=cost(40_000_000, 4_000_000),
        compiler_params=limit(8),
        name="main",
    )(flags, mine, before, after, own_ocean)


def finish(flags, main, halos, rates, wet_blocks, surface_light):
    return pl.pallas_call(
        finish_kernel,
        out_shape=(f32(4, LANES, LANES), bf16(TRACERS, LANES, LANES), f32(LANES, LANES)),
        in_specs=smem(1) + vmem(7) + hbm(3),
        out_specs=hbm(3),
        scratch_shapes=STEP_SCRATCH
        + [
            pltpu.VMEM((2, 12, LEVELS, LANES), jnp.float32),
            pltpu.VMEM((2, ROWS, LEVELS, LANES), jnp.float32),
            pltpu.VMEM((4, ROWS, LEVELS, LANES), jnp.float32),
            pltpu.VMEM((TRACERS, LANES, LANES), jnp.float32),
            pltpu.VMEM((TRACERS, LANES, LANES), jnp.bfloat16),
            pltpu.VMEM((4, LANES, LANES), jnp.float32),
            pltpu.VMEM((LANES, LANES), jnp.float32),
            pltpu.SMEM(rates.shape, jnp.float32),
            pltpu.SMEM(wet_blocks.shape, jnp.int32),
            pltpu.VMEM(surface_light.shape, jnp.float32),
            pltpu.SemaphoreType.DMA((3 + 3 * BLOCKS,)),
        ],
        compiler_params=limit(12),
        name="finish",
    )(flags, *main, *halos, *map(in_hbm, (rates, wet_blocks, surface_light)))


def shards(ocean, tracers, wet_blocks, surface_light, rates):
    tr = tracers.reshape(TRACERS, LANES, LANES)
    oc = ocean.reshape(4, LANES, LANES)
    groups, tiles = lax.axis_size("grp"), lax.axis_size("tile")

    def ahead(x, axis, count):
        return lax.ppermute(x, axis, [(i, i + 1) for i in range(count - 1)])

    def back(x, axis, count):
        return lax.ppermute(x, axis, [(i + 1, i) for i in range(count - 1)])

    g, t = lax.axis_index("grp"), lax.axis_index("tile")
    flags = jnp.stack([g > 0, g < groups - 1, t > 0, t < tiles - 1]).astype(jnp.float32)
    to_next, to_previous, own_ocean, edges = pack(tr, oc)
    from_left = ahead(edges, "tile", tiles)
    before = ahead(to_next, "grp", groups)
    after = back(to_previous, "grp", groups)
    from_right = back(edges, "tile", tiles)
    lane = lax.broadcasted_iota(jnp.int32, (LANES, LANES), 1)
    halo = jnp.where(lane % 8 < 4, from_right, from_left)
    halo_before = ahead(halo[2 * LEVELS :], "grp", groups)
    halo_after = back(halo[: 2 * LEVELS], "grp", groups)
    main = transport(flags, to_next, before, after, own_ocean)
    ocean_out, tracer_out, heating = finish(
        flags, main, (halo, halo_before, halo_after), rates, wet_blocks, surface_light
    )
    return (
        ocean_out.reshape(ocean.shape),
        tracer_out.reshape(tracers.shape),
        heating.reshape(LEVELS, ROWS, LANES),
    )


def solution(mesh):
    return jax.shard_map(
        shards,
        mesh=mesh,
        in_specs=(
            P(None, None, "grp", "tile"),
            P(None, None, "grp", "tile"),
            P("grp", "tile"),
            P("grp", "tile"),
            P(),
        ),
        out_specs=(
            P(None, None, "grp", "tile"),
            P(None, None, "grp", "tile"),
            P(None, "grp", "tile"),
        ),
        check_vma=False,
    )
```

```python
import functools

import functools

import jax
import jax.numpy as jnp
from jax import lax
from jax.experimental import pallas as pl
from jax.experimental.pallas import tpu as pltpu
from jax.sharding import PartitionSpec as P

LEVELS = 32
ROWS = 4
LANES = 128
BLOCKS = LEVELS // 8
GROUP = 24
COPIES = 5
TRACERS = 10

time_step = 0.3
coriolis = 0.2
viscosity = 0.1
diffusion = 0.05
thermal = 0.2
haline = 0.15
gravity_red = 0.05
react_step = 0.5
water_atten = 0.3
chloro_atten = 0.2

U, V, T, S = range(4)
FACES = {}
_count = 0
for _name, _first, _number in (
    ("up1", -2, 8),
    ("um1", -2, 8),
    ("vp1", -3, 9),
    ("vm1", -3, 9),
    ("up2", 0, 4),
    ("um2", 0, 4),
    ("vp2", -1, 5),
    ("vm2", -1, 5),
):
    FACES[_name] = (_count, _first)
    _count += _number
FACE_SLOTS = _count
SPEEDS = {
    key: k
    for k, key in enumerate(
        [("u", "1", j) for j in range(-2, 6)]
        + [("v", "1", j) for j in range(-3, 6)]
        + [("u", "2", j) for j in range(4)]
        + [("v", "2", j) for j in range(-1, 4)]
    )
}
HALO_BEFORE = [(f, j) for f in (U, V) for j in (-3, -2, -1)] + [(f, j) for f in (T, S) for j in (-2, -1)]
HALO_AFTER = [(f, j) for f in (U, V) for j in (4, 5, 6)] + [(f, j) for f in (T, S) for j in (4, 5)]
HALO = {key: k for k, key in enumerate(HALO_BEFORE + HALO_AFTER)}
STRIP = {key: k for k, key in enumerate([(f, j) for f in (U, V) for j in range(-3, 7)] + [(f, j) for f in (T, S) for j in range(-2, 6)])}
PARTS = 2 * 4 * ROWS


def roll(x, shift, axis=1):
    return pltpu.roll(x, shift % x.shape[axis], axis)


def east(x):
    return roll(x, -1)


def west(x):
    return roll(x, 1)


def minmod(a, b):
    return jnp.maximum(jnp.minimum(a, b), jnp.minimum(jnp.maximum(a, b), 0.0))


def rows_of(block, y):
    return pl.ds(block * 8 * ROWS + y, 8, stride=ROWS)


def running_sum(x, sub):
    for step in (1, 2, 4):
        x = x + jnp.where(sub >= step, roll(x, step, 0), 0.0)
    return x


def last_row(x):
    return jnp.broadcast_to(x[7:8, :], x.shape)


def split_speed(faces, axis, stage, j, at, speed):
    for sign, part in (("p", jnp.maximum), ("m", jnp.minimum)):
        slot, first = FACES[axis + sign + stage]
        faces[slot + j - first, at, :] = part(speed, 0.0)


def tendency(q, big, j):
    e = [east(q[f][j]) for f in range(4)]
    w = [west(q[f][j]) for f in range(4)]
    north = [q[f][j + 1] for f in range(4)]
    south = [q[f][j - 1] for f in range(4)]
    half_u, half_v = 0.5 * q[U][j], 0.5 * q[V][j]
    out = []
    for f in range(4):
        advect = half_u * (e[f] - w[f]) + half_v * (north[f] - south[f])
        lap = (e[f] + w[f]) + (north[f] + south[f]) - 4.0 * q[f][j]
        out.append((viscosity if f < 2 else diffusion) * lap - advect)
    press_x = 0.5 * (east(big[j]) - west(big[j]))
    press_y = 0.5 * (big[j + 1] - big[j - 1])
    out[U] = out[U] + coriolis * q[V][j] - press_x
    out[V] = out[V] - coriolis * q[U][j] - press_y
    return out


def ocean_steps(load, put_face, carry, store, up, down, lane_mask):
    sub = lax.broadcasted_iota(jnp.int32, (8, LANES), 0)
    carry[...] = jnp.zeros_like(carry)
    scale = 0.25 * time_step

    def body(block, _):
        at = pl.ds(block * 8, 8)

        def speeds(stage, axis, j, a, b):
            put_face(axis, stage, j, at, scale * (a + b))

        def depth_sum(q, rows, base):
            big = {}
            for j in rows:
                b = (gravity_red * thermal) * q[T][j] - (gravity_red * haline) * q[S][j]
                big[j] = running_sum(b, sub) + carry[base + j]
                carry[base + j] = last_row(big[j])
            return big

        q = [{}, {}, {}, {}]
        for f, j in STRIP:
            q[f][j] = load(f, j, at)
        for j in range(-2, 6):
            speeds("1", "u", j, q[U][j], east(q[U][j]))
        for j in range(-3, 6):
            speeds("1", "v", j, q[V][j], q[V][j + 1])
        big = depth_sum(q, range(-2, 6), 2)
        one = [{}, {}, {}, {}]
        for j in range(-1, 5):
            rate = tendency(q, big, j)
            for f in range(4):
                value = q[f][j] + time_step * rate[f]
                if j < 0:
                    value = value * up
                if j > 3:
                    value = value * down
                if lane_mask is not None:
                    value = value * lane_mask
                one[f][j] = value
        for j in range(4):
            speeds("2", "u", j, one[U][j], east(one[U][j]))
        for j in range(-1, 4):
            speeds("2", "v", j, one[V][j], one[V][j + 1])
        big = depth_sum(one, range(-1, 5), 9)
        for j in range(4):
            rate = tendency(one, big, j)
            for f in range(4):
                store(f, j, at, 0.5 * (q[f][j] + one[f][j] + time_step * rate[f]))
        return 0

    lax.fori_loop(0, BLOCKS, body, 0)


def advance(c, low, high, face, finish):
    diff_before = c(low - 1) - c(low - 2)
    left_before = flux_before = None
    for j in range(low - 1, high + 1):
        here = c(j)
        diff = c(j + 1) - here
        slope = minmod(diff_before, diff)
        twice = here + here
        flux = None
        if left_before is not None:
            flux = face("vp", j - 1) * left_before + face("vm", j - 1) * (twice - slope)
        if flux_before is not None:
            cell = c(j - 1)
            plus, minus, further = east(cell), west(cell), roll(cell, -2)
            d = plus - cell
            s = minmod(cell - minus, d)
            right = (plus + plus) - minmod(d, further - plus)
            fx = face("up", j - 1) * ((cell + cell) + s) + face("um", j - 1) * right
            finish(j - 1, (fx - west(fx)) + (flux - flux_before))
        diff_before, left_before, flux_before = diff, twice + slope, flux


def tracer_steps(load, faces, at, up, down, lane_mask, store):
    def face_of(stage):
        def get(name, j):
            slot, first = FACES[name + stage]
            return faces[slot + j - first, at, :]

        return get

    cells, one = {}, {}

    def cell(j):
        if j not in cells:
            cells[j] = load(j)
        return cells[j]

    def first(j, change):
        value = cell(j) - change
        if j == -1:
            value = value * up
        if j == ROWS:
            value = value * down
        if lane_mask is not None:
            value = value * lane_mask
        one[j] = value.astype(jnp.bfloat16).astype(jnp.float32)

    def second(j, change):
        store(j, 0.5 * ((cell(j) + one[j]) - change))

    advance(cell, -2, ROWS + 2, face_of("1"), first)
    advance(lambda j: one[j], 0, ROWS, face_of("2"), second)


def whole_iota(axis):
    return lax.broadcasted_iota(jnp.int32, (LANES, LANES), axis)


def one_hot(where):
    return jnp.where(where, 1.0, 0.0).astype(jnp.bfloat16)


def level_rows(y):
    return slice(y * LEVELS, (y + 1) * LEVELS)


def part_rows(f, y, part):
    first = TRACERS * LANES + ((f * ROWS + y) * 2 + part) * LEVELS
    return slice(first, first + LEVELS)


def pack_kernel(tr, oc, mine, own_ocean, edges, tracer_in, ocean_in, sems):
    half = pl.ds(0, COPIES), pl.ds(COPIES, COPIES)
    copies = [pltpu.make_async_copy(tr.at[half[k]], tracer_in.at[half[k]], sems.at[k]) for k in range(2)]
    copies.append(pltpu.make_async_copy(oc, ocean_in, sems.at[2]))
    for copy in copies:
        copy.start()
    row, lane = whole_iota(0), whole_iota(1)
    reorder = one_hot(lane == (row % LEVELS) * ROWS + row // LEVELS)
    source = jnp.where(row < 4, row + 8, jnp.where(row >= LANES - 4, row - (LANES - 16), -4 * LANES))
    edge = None

    def with_edges(acc, x, base):
        acc = jnp.where((lane >= base) & (lane < base + 4), roll(x, base), acc)
        return jnp.where((lane >= base + 4) & (lane < base + 8), roll(x, base + 8), acc)

    for k in range(TRACERS):
        if k % COPIES == 0:
            copies[k // COPIES].wait()
        x = jnp.dot(reorder, tracer_in[k], preferred_element_type=jnp.float32)
        mine[k * LANES : (k + 1) * LANES, :] = x.astype(jnp.bfloat16)
        here = GROUP * (k % COPIES) + 8 * (k // COPIES)
        term = jnp.dot(tracer_in[k], one_hot(lane == source + here), preferred_element_type=jnp.float32)
        edge = term if edge is None else edge + term
    acc = jnp.dot(reorder, edge.astype(jnp.bfloat16), preferred_element_type=jnp.float32)
    copies[2].wait()
    for f in range(4):
        for y in range(ROWS):
            x = ocean_in[f, pl.ds(y, LEVELS, stride=ROWS), :]
            own_ocean[f, level_rows(y), :] = x
            high = x.astype(jnp.bfloat16)
            mine[part_rows(f, y, 0), :] = high
            mine[part_rows(f, y, 1), :] = (x - high.astype(jnp.float32)).astype(jnp.bfloat16)
        acc = with_edges(acc, own_ocean[f], GROUP * f)
    edges[...] = acc


def main_kernel(flags, mine, near, far, own_ocean, two, ocean_two, strip, ocean_strip, faces, carry, halo):
    up, down, even = flags[0], flags[1], flags[4] > 0.5

    def side(tile, at):
        if tile == 1:
            return mine[at, :]
        first, second = (far, near) if tile == 0 else (near, far)
        return jnp.where(even, first[at, :], second[at, :])

    for (f, j), k in HALO.items():
        parts = [side((j + ROWS) // ROWS, part_rows(f, j % ROWS, part)).astype(jnp.float32) for part in range(2)]
        halo[k] = parts[0] + parts[1]

    def load(f, j, at):
        if 0 <= j < ROWS:
            return own_ocean[f, pl.ds(at.start + j * LEVELS, 8), :]
        return halo[HALO[f, j], at, :]

    def store(f, j, at, value):
        ocean_two[f, j, at, :] = value

    ocean_steps(load, functools.partial(split_speed, faces), carry, store, up, down, None)

    def body(t, _):
        for part in range(LEVELS // 16):
            for half in range(2):

                def cell(j):
                    y = (j + 4) % 4
                    at = pl.multiple_of(t * LANES + y * LEVELS + part * 16, 16)
                    return side((j + 4) // 4, pl.ds(at, 16)).astype(jnp.float32)[half * 8 : half * 8 + 8]

                at = slice(part * 16 + half * 8, part * 16 + half * 8 + 8)

                def put(j, value):
                    two[t, j, at, :] = value

                tracer_steps(cell, faces, at, up, down, None, put)
        return 0

    lax.fori_loop(0, TRACERS, body, 0)

    row, lane = whole_iota(0), whole_iota(1)
    source = jnp.where(row >= LANES - 8, row - (LANES - 8), jnp.where(row < 8, row + 16, -LANES * 4))
    picks = [one_hot(lane == source + GROUP * k) for k in range(COPIES)]
    for tile in range(3):
        for half in range(2):
            acc = None
            for k in range(COPIES):
                at = (half * COPIES + k) * LANES
                term = jnp.dot(side(tile, slice(at, at + LANES)), picks[k], preferred_element_type=jnp.float32)
                acc = term if acc is None else acc + term
            strip[half, tile] = acc
    lanes = lax.broadcasted_iota(jnp.int32, (LEVELS, LANES), 1)
    for (f, j), k in STRIP.items():
        x = own_ocean[f, level_rows(j), :] if 0 <= j < ROWS else halo[HALO[f, j]]
        x = jnp.where(lanes < 8, roll(x, 8), roll(x, 16))
        ocean_strip[k] = jnp.where((lanes < 8) | ((lanes >= 16) & (lanes < 24)), x, 0.0)


def finish_kernel(
    flags, two, ocean_two, strip, ocean_strip, from_left, from_right, rates_in, wet_in, light_in,
    ocean_out, tracer_out, heating, faces, carry, raw, halo, cells, strip_two, strip_ocean, reacted, narrow, ocean_done, heat_done,
    rates, wet_blocks, light, sems,
):
    small = [
        pltpu.make_async_copy(source, target, sems.at[k])
        for k, (source, target) in enumerate(((rates_in, rates), (wet_in, wet_blocks), (light_in, light)))
    ]
    for copy in small:
        copy.start()
    up, down, left, right = (flags[k] for k in range(4))
    lanes = lax.broadcasted_iota(jnp.int32, (LEVELS, LANES), 1)

    from_one = lax.broadcasted_iota(jnp.int32, halo.shape, 1) % 8 < 4
    halo[...] = jnp.where(from_one, from_right[...], from_left[...])

    middle = (lanes % GROUP >= 8) & (lanes % GROUP < 16)
    for j in range(-4, 8):
        tile, y = (j + 4) // 4, (j + 4) % 4
        for half in range(2):
            x = strip[half, tile, level_rows(y), :]
            if -2 <= j < 6:
                fresh = halo[level_rows(j + 2), :]
                x = jnp.where(middle, roll(fresh, -8) if half else fresh, x)
            cells[half, j + 4] = x

    place_in = lax.broadcasted_iota(jnp.int32, (8, LANES), 1)
    first_middle = (place_in >= 8) & (place_in < 16)
    place_in = place_in % GROUP
    lane_mask = jnp.where((place_in >= 8) & (place_in < 12), right, jnp.where((place_in >= 12) & (place_in < 16), left, 1.0))

    def load(f, j, at):
        x = ocean_strip[STRIP[f, j], at, :]
        if -2 <= j < 6:
            fresh = halo[pl.ds(at.start + (j + 2) * LEVELS, 8), :]
            x = jnp.where(first_middle, roll(fresh, 8 - GROUP * f), x)
        return x

    def store(f, j, at, value):
        strip_ocean[f, j, at, :] = value

    def keep(axis, stage, j, at, speed):
        raw[SPEEDS[axis, stage, j], at, :] = speed

    ocean_steps(load, keep, carry, store, up, down, lane_mask)
    row, whole_lane = whole_iota(0), whole_iota(1)
    copy_out = one_hot((row < GROUP) & (whole_lane % GROUP == row) & (whole_lane < GROUP * COPIES))
    copy_out = jnp.concatenate([copy_out, copy_out], axis=0)
    for axis, stage, j in SPEEDS:
        x = raw[SPEEDS[axis, stage, j]]
        high = x.astype(jnp.bfloat16)
        low = (x - high.astype(jnp.float32)).astype(jnp.bfloat16)
        speed = jnp.dot(jnp.concatenate([high, low], axis=1), copy_out, preferred_element_type=jnp.float32)
        split_speed(faces, axis, stage, j, slice(0, LEVELS), speed)

    def body(block, _):
        at = pl.ds(block * 8, 8)
        for half in range(2):

            def put(j, value):
                strip_two[half, j, at, :] = value

            tracer_steps(lambda j: cells[half, j + 4, at, :], faces, at, up, down, lane_mask, put)
        return 0

    lax.fori_loop(0, BLOCKS, body, 0, unroll=2)
    for copy in small:
        copy.wait()
    lane = lax.broadcasted_iota(jnp.int32, (8, LANES), 1)
    sub = lax.broadcasted_iota(jnp.int32, (8, LANES), 0)
    wet = jnp.zeros((8, LANES), jnp.float32)
    for k in range(8):
        wet = jnp.where(lane // 16 == k, wet_blocks[0, k].astype(jnp.float32), wet)
    half_wet = react_step * wet

    def patched(x, edge, base):
        x = jnp.where(lane >= LANES - 4, roll(edge, 120 - base), x)
        return jnp.where(lane < 4, roll(edge, -16 - base), x)

    def results(block):
        rows = pl.ds(pl.multiple_of(block * 8 * ROWS, 8 * ROWS), 8 * ROWS)
        return (
            pltpu.make_async_copy(narrow.at[:, rows, :], tracer_out.at[:, rows, :], sems.at[3 + block]),
            pltpu.make_async_copy(ocean_done.at[:, rows, :], ocean_out.at[:, rows, :], sems.at[3 + BLOCKS + block]),
            pltpu.make_async_copy(heat_done.at[rows, :], heating.at[rows, :], sems.at[3 + 2 * BLOCKS + block]),
        )

    def last(block, sums):
        sums = list(sums)
        at = pl.ds(block * 8, 8)
        for pair in range(0, ROWS, 2):
            ys = (pair, pair + 1)
            edge = {y: [strip_two[half, y, at, :] for half in range(2)] for y in ys}
            c = {
                y: [patched(two[t, y, at, :], edge[y][t // COPIES], GROUP * (t % COPIES)) for t in range(TRACERS)]
                for y in ys
            }
            att = {}
            for a in range(TRACERS):
                total = {}
                for b in range(TRACERS):
                    rate = rates[a, b]
                    for y in ys:
                        term = rate * c[y][b]
                        total[y] = term if b == 0 else total[y] + term
                for y in ys:
                    value = c[y][a] + half_wet * total[y]
                    reacted[a, rows_of(block, y), :] = value
                    if a == 0:
                        att[y] = water_atten + chloro_atten * value * value
            for y in ys:
                cum = running_sum(att[y], sub) + sums[y]
                sums[y] = last_row(cum)
                heat = wet * light[y : y + 1, :] * (jnp.exp(att[y] - cum) - jnp.exp(-cum))
                heat_done[rows_of(block, y), :] = heat
                for f in range(4):
                    value = patched(ocean_two[f, y, at, :], strip_ocean[f, y, at, :], 0)
                    if f == T:
                        value = value + time_step * heat
                    ocean_done[f, rows_of(block, y), :] = value
        rows = pl.ds(pl.multiple_of(block * 8 * ROWS, 8 * ROWS), 8 * ROWS)
        narrow[:, rows, :] = reacted[:, rows, :].astype(jnp.bfloat16)
        for copy in results(block):
            copy.start()
        return tuple(sums)

    zero = jnp.zeros((8, LANES), jnp.float32)
    lax.fori_loop(0, BLOCKS, last, (zero,) * ROWS)
    for block in range(BLOCKS):
        for copy in results(block):
            copy.wait()


def vmem(count):
    return [pl.BlockSpec(memory_space=pltpu.VMEM)] * count


def smem(count):
    return [pl.BlockSpec(memory_space=pltpu.SMEM)] * count


def hbm(count):
    return [pl.BlockSpec(memory_space=pltpu.HBM)] * count


def in_hbm(x):
    return pltpu.with_memory_space_constraint(x, pltpu.HBM)


def f32(*shape):
    return jax.ShapeDtypeStruct(shape, jnp.float32)


def bf16(*shape):
    return jax.ShapeDtypeStruct(shape, jnp.bfloat16)


def limit(mib):
    return pltpu.CompilerParams(vmem_limit_bytes=mib << 20)


def cost(flops, size):
    return pl.CostEstimate(flops=flops, bytes_accessed=size, transcendentals=0)


STEP_SCRATCH = [
    pltpu.VMEM((FACE_SLOTS, LEVELS, LANES), jnp.float32),
    pltpu.VMEM((14, 8, LANES), jnp.float32),
]


def pack(tr, oc):
    payload = TRACERS * LANES + PARTS * LEVELS
    return pl.pallas_call(
        pack_kernel,
        out_shape=(bf16(payload, LANES), f32(4, LANES, LANES), f32(LANES, LANES)),
        in_specs=hbm(2),
        out_specs=vmem(3),
        scratch_shapes=[
            pltpu.VMEM((TRACERS, LANES, LANES), jnp.bfloat16),
            pltpu.VMEM((4, LANES, LANES), jnp.float32),
            pltpu.SemaphoreType.DMA((3,)),
        ],
        compiler_params=limit(8),
        name="pack",
    )(in_hbm(tr), in_hbm(oc))


def transport(flags, mine, near, far, own_ocean):
    return pl.pallas_call(
        main_kernel,
        out_shape=(
            f32(TRACERS, ROWS, LEVELS, LANES),
            f32(4, ROWS, LEVELS, LANES),
            f32(2, 3, LANES, LANES),
            f32(len(STRIP), LEVELS, LANES),
        ),
        in_specs=smem(1) + vmem(4),
        out_specs=vmem(4),
        scratch_shapes=STEP_SCRATCH + [pltpu.VMEM((len(HALO), LEVELS, LANES), jnp.float32)],
        cost_estimate=cost(40_000_000, 4_000_000),
        compiler_params=limit(8),
        name="main",
    )(flags, mine, near, far, own_ocean)


def finish(flags, main, halos, rates, wet_blocks, surface_light):
    return pl.pallas_call(
        finish_kernel,
        out_shape=(f32(4, LANES, LANES), bf16(TRACERS, LANES, LANES), f32(LANES, LANES)),
        in_specs=smem(1) + vmem(6) + hbm(3),
        out_specs=hbm(3),
        scratch_shapes=STEP_SCRATCH
        + [
            pltpu.VMEM((len(SPEEDS), LEVELS, LANES), jnp.float32),
            pltpu.VMEM((2 * LANES, LANES), jnp.float32),
            pltpu.VMEM((2, 12, LEVELS, LANES), jnp.float32),
            pltpu.VMEM((2, ROWS, LEVELS, LANES), jnp.float32),
            pltpu.VMEM((4, ROWS, LEVELS, LANES), jnp.float32),
            pltpu.VMEM((TRACERS, LANES, LANES), jnp.float32),
            pltpu.VMEM((TRACERS, LANES, LANES), jnp.bfloat16),
            pltpu.VMEM((4, LANES, LANES), jnp.float32),
            pltpu.VMEM((LANES, LANES), jnp.float32),
            pltpu.SMEM(rates.shape, jnp.float32),
            pltpu.SMEM(wet_blocks.shape, jnp.int32),
            pltpu.VMEM(surface_light.shape, jnp.float32),
            pltpu.SemaphoreType.DMA((3 + 3 * BLOCKS,)),
        ],
        compiler_params=limit(12),
        name="finish",
    )(flags, *main, *halos, *map(in_hbm, (rates, wet_blocks, surface_light)))


def shards(ocean, tracers, wet_blocks, surface_light, rates):
    tr = tracers.reshape(TRACERS, LANES, LANES)
    oc = ocean.reshape(4, LANES, LANES)
    groups, tiles = lax.axis_size("grp"), lax.axis_size("tile")

    def ahead(x, axis, count):
        return lax.ppermute(x, axis, [(i, i + 1) for i in range(count - 1)])

    def back(x, axis, count):
        return lax.ppermute(x, axis, [(i + 1, i) for i in range(count - 1)])

    within = [(i, i ^ 1) for i in range(groups) if i ^ 1 < groups]
    between = [pair for i in range(1, groups - 1, 2) for pair in ((i, i + 1), (i + 1, i))]
    g, t = lax.axis_index("grp"), lax.axis_index("tile")
    flags = jnp.stack([g > 0, g < groups - 1, t > 0, t < tiles - 1, g % 2 == 0]).astype(jnp.float32)
    mine, own_ocean, edges = pack(tr, oc)
    edges_far = lax.ppermute(edges, "grp", between)
    edges_near = lax.ppermute(edges, "grp", within)
    far = lax.ppermute(mine, "grp", between)
    near = lax.ppermute(mine, "grp", within)
    even, half = g % 2 == 0, 2 * LEVELS
    edges_before = jnp.where(even, edges_far[half:], edges_near[half:])
    edges_after = jnp.where(even, edges_near[:half], edges_far[:half])
    edges = jnp.concatenate([edges_before, edges, edges_after], axis=0)
    from_left = ahead(edges, "tile", tiles)
    from_right = back(edges, "tile", tiles)
    main = transport(flags, mine, near, far, own_ocean)
    ocean_out, tracer_out, heating = finish(
        flags, main, (from_left, from_right), rates, wet_blocks, surface_light
    )
    return (
        ocean_out.reshape(ocean.shape),
        tracer_out.reshape(tracers.shape),
        heating.reshape(LEVELS, ROWS, LANES),
    )


def solution(mesh):
    return jax.shard_map(
        shards,
        mesh=mesh,
        in_specs=(
            P(None, None, "grp", "tile"),
            P(None, None, "grp", "tile"),
            P("grp", "tile"),
            P("grp", "tile"),
            P(),
        ),
        out_specs=(
            P(None, None, "grp", "tile"),
            P(None, None, "grp", "tile"),
            P(None, "grp", "tile"),
        ),
        check_vma=False,
    )
```

```python
import functools

import functools

import jax
import jax.numpy as jnp
from jax import lax
from jax.experimental import pallas as pl
from jax.experimental.pallas import tpu as pltpu
from jax.sharding import PartitionSpec as P

LEVELS = 32
ROWS = 4
LANES = 128
BLOCKS = LEVELS // 8
GROUP = 24
COPIES = 5
TRACERS = 10

time_step = 0.3
coriolis = 0.2
viscosity = 0.1
diffusion = 0.05
thermal = 0.2
haline = 0.15
gravity_red = 0.05
react_step = 0.5
water_atten = 0.3
chloro_atten = 0.2

U, V, T, S = range(4)
FACES = {}
_count = 0
for _name, _first, _number in (
    ("up1", -2, 8),
    ("um1", -2, 8),
    ("vp1", -3, 9),
    ("vm1", -3, 9),
    ("up2", 0, 4),
    ("um2", 0, 4),
    ("vp2", -1, 5),
    ("vm2", -1, 5),
):
    FACES[_name] = (_count, _first)
    _count += _number
FACE_SLOTS = _count
SPEEDS = {
    key: k
    for k, key in enumerate(
        [("u", "1", j) for j in range(-2, 6)]
        + [("v", "1", j) for j in range(-3, 6)]
        + [("u", "2", j) for j in range(4)]
        + [("v", "2", j) for j in range(-1, 4)]
    )
}
HALO_BEFORE = [(f, j) for f in (U, V) for j in (-3, -2, -1)] + [(f, j) for f in (T, S) for j in (-2, -1)]
HALO_AFTER = [(f, j) for f in (U, V) for j in (4, 5, 6)] + [(f, j) for f in (T, S) for j in (4, 5)]
HALO = {key: k for k, key in enumerate(HALO_BEFORE + HALO_AFTER)}
STRIP = {key: k for k, key in enumerate([(f, j) for f in (U, V) for j in range(-3, 7)] + [(f, j) for f in (T, S) for j in range(-2, 6)])}
PARTS = 2 * 4 * ROWS


def roll(x, shift, axis=1):
    return pltpu.roll(x, shift % x.shape[axis], axis)


def east(x):
    return roll(x, -1)


def west(x):
    return roll(x, 1)


def minmod(a, b):
    return jnp.maximum(jnp.minimum(a, b), jnp.minimum(jnp.maximum(a, b), 0.0))


def rows_of(block, y):
    return pl.ds(block * 8 * ROWS + y, 8, stride=ROWS)


def running_sum(x, sub):
    for step in (1, 2, 4):
        x = x + jnp.where(sub >= step, roll(x, step, 0), 0.0)
    return x


def last_row(x):
    return jnp.broadcast_to(x[7:8, :], x.shape)


def split_speed(faces, axis, stage, j, at, speed):
    for sign, part in (("p", jnp.maximum), ("m", jnp.minimum)):
        slot, first = FACES[axis + sign + stage]
        faces[slot + j - first, at, :] = part(speed, 0.0)


def tendency(q, big, j):
    e = [east(q[f][j]) for f in range(4)]
    w = [west(q[f][j]) for f in range(4)]
    north = [q[f][j + 1] for f in range(4)]
    south = [q[f][j - 1] for f in range(4)]
    half_u, half_v = 0.5 * q[U][j], 0.5 * q[V][j]
    out = []
    for f in range(4):
        advect = half_u * (e[f] - w[f]) + half_v * (north[f] - south[f])
        lap = (e[f] + w[f]) + (north[f] + south[f]) - 4.0 * q[f][j]
        out.append((viscosity if f < 2 else diffusion) * lap - advect)
    press_x = 0.5 * (east(big[j]) - west(big[j]))
    press_y = 0.5 * (big[j + 1] - big[j - 1])
    out[U] = out[U] + coriolis * q[V][j] - press_x
    out[V] = out[V] - coriolis * q[U][j] - press_y
    return out


def ocean_steps(load, put_face, carry, store, up, down, lane_mask):
    sub = lax.broadcasted_iota(jnp.int32, (8, LANES), 0)
    carry[...] = jnp.zeros_like(carry)
    scale = 0.25 * time_step

    def body(block, _):
        at = pl.ds(block * 8, 8)

        def speeds(stage, axis, j, a, b):
            put_face(axis, stage, j, at, scale * (a + b))

        def depth_sum(q, rows, base):
            big = {}
            for j in rows:
                b = (gravity_red * thermal) * q[T][j] - (gravity_red * haline) * q[S][j]
                big[j] = running_sum(b, sub) + carry[base + j]
                carry[base + j] = last_row(big[j])
            return big

        q = [{}, {}, {}, {}]
        for f, j in STRIP:
            q[f][j] = load(f, j, at)
        for j in range(-2, 6):
            speeds("1", "u", j, q[U][j], east(q[U][j]))
        for j in range(-3, 6):
            speeds("1", "v", j, q[V][j], q[V][j + 1])
        big = depth_sum(q, range(-2, 6), 2)
        one = [{}, {}, {}, {}]
        for j in range(-1, 5):
            rate = tendency(q, big, j)
            for f in range(4):
                value = q[f][j] + time_step * rate[f]
                if j < 0:
                    value = value * up
                if j > 3:
                    value = value * down
                if lane_mask is not None:
                    value = value * lane_mask
                one[f][j] = value
        for j in range(4):
            speeds("2", "u", j, one[U][j], east(one[U][j]))
        for j in range(-1, 4):
            speeds("2", "v", j, one[V][j], one[V][j + 1])
        big = depth_sum(one, range(-1, 5), 9)
        for j in range(4):
            rate = tendency(one, big, j)
            for f in range(4):
                store(f, j, at, 0.5 * (q[f][j] + one[f][j] + time_step * rate[f]))
        return 0

    lax.fori_loop(0, BLOCKS, body, 0, unroll=2)


def advance(c, low, high, face, finish):
    diff_before = c(low - 1) - c(low - 2)
    left_before = flux_before = None
    for j in range(low - 1, high + 1):
        here = c(j)
        diff = c(j + 1) - here
        slope = minmod(diff_before, diff)
        twice = here + here
        flux = None
        if left_before is not None:
            flux = face("vp", j - 1) * left_before + face("vm", j - 1) * (twice - slope)
        if flux_before is not None:
            cell = c(j - 1)
            plus, minus, further = east(cell), west(cell), roll(cell, -2)
            d = plus - cell
            s = minmod(cell - minus, d)
            right = (plus + plus) - minmod(d, further - plus)
            fx = face("up", j - 1) * ((cell + cell) + s) + face("um", j - 1) * right
            finish(j - 1, (fx - west(fx)) + (flux - flux_before))
        diff_before, left_before, flux_before = diff, twice + slope, flux


def tracer_steps(load, faces, at, up, down, lane_mask, store):
    def face_of(stage):
        def get(name, j):
            slot, first = FACES[name + stage]
            return faces[slot + j - first, at, :]

        return get

    cells, one = {}, {}

    def cell(j):
        if j not in cells:
            cells[j] = load(j)
        return cells[j]

    def first(j, change):
        value = cell(j) - change
        if j == -1:
            value = value * up
        if j == ROWS:
            value = value * down
        if lane_mask is not None:
            value = value * lane_mask
        one[j] = value.astype(jnp.bfloat16).astype(jnp.float32)

    def second(j, change):
        store(j, 0.5 * ((cell(j) + one[j]) - change))

    advance(cell, -2, ROWS + 2, face_of("1"), first)
    advance(lambda j: one[j], 0, ROWS, face_of("2"), second)


def whole_iota(axis):
    return lax.broadcasted_iota(jnp.int32, (LANES, LANES), axis)


def one_hot(where):
    return jnp.where(where, 1.0, 0.0).astype(jnp.bfloat16)


def level_rows(y):
    return slice(y * LEVELS, (y + 1) * LEVELS)


def part_rows(f, y, part):
    first = TRACERS * LANES + ((f * ROWS + y) * 2 + part) * LEVELS
    return slice(first, first + LEVELS)


def pack_kernel(tr, oc, mine, own_ocean, edges, tracer_in, ocean_in, sems):
    half = pl.ds(0, COPIES), pl.ds(COPIES, COPIES)
    copies = [pltpu.make_async_copy(tr.at[half[k]], tracer_in.at[half[k]], sems.at[k]) for k in range(2)]
    copies.append(pltpu.make_async_copy(oc, ocean_in, sems.at[2]))
    for copy in copies:
        copy.start()
    row, lane = whole_iota(0), whole_iota(1)
    reorder = one_hot(lane == (row % LEVELS) * ROWS + row // LEVELS)
    source = jnp.where(row < 4, row + 8, jnp.where(row >= LANES - 4, row - (LANES - 16), -4 * LANES))
    edge = None

    def with_edges(acc, x, base):
        acc = jnp.where((lane >= base) & (lane < base + 4), roll(x, base), acc)
        return jnp.where((lane >= base + 4) & (lane < base + 8), roll(x, base + 8), acc)

    for k in range(TRACERS):
        if k % COPIES == 0:
            copies[k // COPIES].wait()
        x = jnp.dot(reorder, tracer_in[k], preferred_element_type=jnp.float32)
        mine[k * LANES : (k + 1) * LANES, :] = x.astype(jnp.bfloat16)
        here = GROUP * (k % COPIES) + 8 * (k // COPIES)
        term = jnp.dot(tracer_in[k], one_hot(lane == source + here), preferred_element_type=jnp.float32)
        edge = term if edge is None else edge + term
    acc = jnp.dot(reorder, edge.astype(jnp.bfloat16), preferred_element_type=jnp.float32)
    copies[2].wait()
    for f in range(4):
        for y in range(ROWS):
            x = ocean_in[f, pl.ds(y, LEVELS, stride=ROWS), :]
            own_ocean[f, level_rows(y), :] = x
            high = x.astype(jnp.bfloat16)
            mine[part_rows(f, y, 0), :] = high
            mine[part_rows(f, y, 1), :] = (x - high.astype(jnp.float32)).astype(jnp.bfloat16)
        acc = with_edges(acc, own_ocean[f], GROUP * f)
    edges[...] = acc


def main_kernel(flags, mine, near, far, own_ocean, two, ocean_two, strip, ocean_strip, faces, carry, halo):
    up, down, even = flags[0], flags[1], flags[4] > 0.5

    def side(tile, at):
        if tile == 1:
            return mine[at, :]
        first, second = (far, near) if tile == 0 else (near, far)
        return jnp.where(even, first[at, :], second[at, :])

    for (f, j), k in HALO.items():
        parts = [side((j + ROWS) // ROWS, part_rows(f, j % ROWS, part)).astype(jnp.float32) for part in range(2)]
        halo[k] = parts[0] + parts[1]

    def load(f, j, at):
        if 0 <= j < ROWS:
            return own_ocean[f, pl.ds(at.start + j * LEVELS, 8), :]
        return halo[HALO[f, j], at, :]

    def store(f, j, at, value):
        ocean_two[f, j, at, :] = value

    ocean_steps(load, functools.partial(split_speed, faces), carry, store, up, down, None)

    def body(t, _):
        for part in range(LEVELS // 16):
            for half in range(2):

                def cell(j):
                    y = (j + 4) % 4
                    at = pl.multiple_of(t * LANES + y * LEVELS + part * 16, 16)
                    return side((j + 4) // 4, pl.ds(at, 16)).astype(jnp.float32)[half * 8 : half * 8 + 8]

                at = slice(part * 16 + half * 8, part * 16 + half * 8 + 8)

                def put(j, value):
                    two[t, j, at, :] = value

                tracer_steps(cell, faces, at, up, down, None, put)
        return 0

    lax.fori_loop(0, TRACERS, body, 0)

    row, lane = whole_iota(0), whole_iota(1)
    source = jnp.where(row >= LANES - 8, row - (LANES - 8), jnp.where(row < 8, row + 16, -LANES * 4))
    picks = [one_hot(lane == source + GROUP * k) for k in range(COPIES)]
    for tile in range(3):
        for half in range(2):
            acc = None
            for k in range(COPIES):
                at = (half * COPIES + k) * LANES
                term = jnp.dot(side(tile, slice(at, at + LANES)), picks[k], preferred_element_type=jnp.float32)
                acc = term if acc is None else acc + term
            strip[half, tile] = acc
    lanes = lax.broadcasted_iota(jnp.int32, (LEVELS, LANES), 1)
    for (f, j), k in STRIP.items():
        x = own_ocean[f, level_rows(j), :] if 0 <= j < ROWS else halo[HALO[f, j]]
        x = jnp.where(lanes < 8, roll(x, 8), roll(x, 16))
        ocean_strip[k] = jnp.where((lanes < 8) | ((lanes >= 16) & (lanes < 24)), x, 0.0)


def finish_kernel(
    flags, two, ocean_two, strip, ocean_strip, from_left, from_right, rates_in, wet_in, light_in,
    ocean_out, tracer_out, heating, faces, carry, raw, halo, cells, strip_two, strip_ocean, reacted, narrow, ocean_done, heat_done,
    rates, wet_blocks, light, sems,
):
    small = [
        pltpu.make_async_copy(source, target, sems.at[k])
        for k, (source, target) in enumerate(((rates_in, rates), (wet_in, wet_blocks), (light_in, light)))
    ]
    for copy in small:
        copy.start()
    up, down, left, right = (flags[k] for k in range(4))
    lanes = lax.broadcasted_iota(jnp.int32, (LEVELS, LANES), 1)

    from_one = lax.broadcasted_iota(jnp.int32, halo.shape, 1) % 8 < 4
    halo[...] = jnp.where(from_one, from_right[...], from_left[...])

    middle = (lanes % GROUP >= 8) & (lanes % GROUP < 16)
    for j in range(-4, 8):
        tile, y = (j + 4) // 4, (j + 4) % 4
        for half in range(2):
            x = strip[half, tile, level_rows(y), :]
            if -2 <= j < 6:
                fresh = halo[level_rows(j + 2), :]
                x = jnp.where(middle, roll(fresh, -8) if half else fresh, x)
            cells[half, j + 4] = x

    place_in = lax.broadcasted_iota(jnp.int32, (8, LANES), 1)
    first_middle = (place_in >= 8) & (place_in < 16)
    place_in = place_in % GROUP
    lane_mask = jnp.where((place_in >= 8) & (place_in < 12), right, jnp.where((place_in >= 12) & (place_in < 16), left, 1.0))

    def load(f, j, at):
        x = ocean_strip[STRIP[f, j], at, :]
        if -2 <= j < 6:
            fresh = halo[pl.ds(at.start + (j + 2) * LEVELS, 8), :]
            x = jnp.where(first_middle, roll(fresh, 8 - GROUP * f), x)
        return x

    def store(f, j, at, value):
        strip_ocean[f, j, at, :] = value

    def keep(axis, stage, j, at, speed):
        raw[SPEEDS[axis, stage, j], at, :] = speed

    ocean_steps(load, keep, carry, store, up, down, lane_mask)
    row, whole_lane = whole_iota(0), whole_iota(1)
    copy_out = one_hot((row < GROUP) & (whole_lane % GROUP == row) & (whole_lane < GROUP * COPIES))
    copy_out = jnp.concatenate([copy_out, copy_out], axis=0)
    names = list(SPEEDS)
    for first in range(0, len(names), 13):
        x = jnp.concatenate([raw[k] for k in range(first, first + 13)], axis=0)
        high = x.astype(jnp.bfloat16)
        low = (x - high.astype(jnp.float32)).astype(jnp.bfloat16)
        speed = jnp.dot(jnp.concatenate([high, low], axis=1), copy_out, preferred_element_type=jnp.float32)
        for k in range(13):
            split_speed(faces, *names[first + k], slice(0, LEVELS), speed[k * LEVELS : (k + 1) * LEVELS])

    def body(block, _):
        at = pl.ds(block * 8, 8)
        for half in range(2):

            def put(j, value):
                strip_two[half, j, at, :] = value

            tracer_steps(lambda j: cells[half, j + 4, at, :], faces, at, up, down, lane_mask, put)
        return 0

    lax.fori_loop(0, BLOCKS, body, 0, unroll=2)
    for copy in small:
        copy.wait()
    lane = lax.broadcasted_iota(jnp.int32, (8, LANES), 1)
    sub = lax.broadcasted_iota(jnp.int32, (8, LANES), 0)
    wet = jnp.zeros((8, LANES), jnp.float32)
    for k in range(8):
        wet = jnp.where(lane // 16 == k, wet_blocks[0, k].astype(jnp.float32), wet)
    half_wet = react_step * wet

    def patched(x, edge, base):
        x = jnp.where(lane >= LANES - 4, roll(edge, 120 - base), x)
        return jnp.where(lane < 4, roll(edge, -16 - base), x)

    def results(block):
        rows = pl.ds(pl.multiple_of(block * 8 * ROWS, 8 * ROWS), 8 * ROWS)
        return (
            pltpu.make_async_copy(narrow.at[:, rows, :], tracer_out.at[:, rows, :], sems.at[3 + block]),
            pltpu.make_async_copy(ocean_done.at[:, rows, :], ocean_out.at[:, rows, :], sems.at[3 + BLOCKS + block]),
            pltpu.make_async_copy(heat_done.at[rows, :], heating.at[rows, :], sems.at[3 + 2 * BLOCKS + block]),
        )

    def last(block, sums):
        sums = list(sums)
        at = pl.ds(block * 8, 8)
        for pair in range(0, ROWS, 2):
            ys = (pair, pair + 1)
            edge = {y: [strip_two[half, y, at, :] for half in range(2)] for y in ys}
            c = {
                y: [patched(two[t, y, at, :], edge[y][t // COPIES], GROUP * (t % COPIES)) for t in range(TRACERS)]
                for y in ys
            }
            att = {}
            for a in range(TRACERS):
                total = {}
                for b in range(TRACERS):
                    rate = rates[a, b]
                    for y in ys:
                        term = rate * c[y][b]
                        total[y] = term if b == 0 else total[y] + term
                for y in ys:
                    value = c[y][a] + half_wet * total[y]
                    reacted[a, rows_of(block, y), :] = value
                    if a == 0:
                        att[y] = water_atten + chloro_atten * value * value
            for y in ys:
                cum = running_sum(att[y], sub) + sums[y]
                sums[y] = last_row(cum)
                heat = wet * light[y : y + 1, :] * (jnp.exp(att[y] - cum) - jnp.exp(-cum))
                heat_done[rows_of(block, y), :] = heat
                for f in range(4):
                    value = patched(ocean_two[f, y, at, :], strip_ocean[f, y, at, :], 0)
                    if f == T:
                        value = value + time_step * heat
                    ocean_done[f, rows_of(block, y), :] = value
        rows = pl.ds(pl.multiple_of(block * 8 * ROWS, 8 * ROWS), 8 * ROWS)
        narrow[:, rows, :] = reacted[:, rows, :].astype(jnp.bfloat16)
        for copy in results(block):
            copy.start()
        return tuple(sums)

    zero = jnp.zeros((8, LANES), jnp.float32)
    lax.fori_loop(0, BLOCKS, last, (zero,) * ROWS)
    for block in range(BLOCKS):
        for copy in results(block):
            copy.wait()


def vmem(count):
    return [pl.BlockSpec(memory_space=pltpu.VMEM)] * count


def smem(count):
    return [pl.BlockSpec(memory_space=pltpu.SMEM)] * count


def hbm(count):
    return [pl.BlockSpec(memory_space=pltpu.HBM)] * count


def in_hbm(x):
    return pltpu.with_memory_space_constraint(x, pltpu.HBM)


def f32(*shape):
    return jax.ShapeDtypeStruct(shape, jnp.float32)


def bf16(*shape):
    return jax.ShapeDtypeStruct(shape, jnp.bfloat16)


def limit(mib):
    return pltpu.CompilerParams(vmem_limit_bytes=mib << 20)


def cost(flops, size):
    return pl.CostEstimate(flops=flops, bytes_accessed=size, transcendentals=0)


STEP_SCRATCH = [
    pltpu.VMEM((FACE_SLOTS, LEVELS, LANES), jnp.float32),
    pltpu.VMEM((14, 8, LANES), jnp.float32),
]


def pack(tr, oc):
    payload = TRACERS * LANES + PARTS * LEVELS
    return pl.pallas_call(
        pack_kernel,
        out_shape=(bf16(payload, LANES), f32(4, LANES, LANES), f32(LANES, LANES)),
        in_specs=hbm(2),
        out_specs=vmem(3),
        scratch_shapes=[
            pltpu.VMEM((TRACERS, LANES, LANES), jnp.bfloat16),
            pltpu.VMEM((4, LANES, LANES), jnp.float32),
            pltpu.SemaphoreType.DMA((3,)),
        ],
        compiler_params=limit(8),
        name="pack",
    )(in_hbm(tr), in_hbm(oc))


def transport(flags, mine, near, far, own_ocean):
    return pl.pallas_call(
        main_kernel,
        out_shape=(
            f32(TRACERS, ROWS, LEVELS, LANES),
            f32(4, ROWS, LEVELS, LANES),
            f32(2, 3, LANES, LANES),
            f32(len(STRIP), LEVELS, LANES),
        ),
        in_specs=smem(1) + vmem(4),
        out_specs=vmem(4),
        scratch_shapes=STEP_SCRATCH + [pltpu.VMEM((len(HALO), LEVELS, LANES), jnp.float32)],
        cost_estimate=cost(40_000_000, 4_000_000),
        compiler_params=limit(8),
        name="main",
    )(flags, mine, near, far, own_ocean)


def finish(flags, main, halos, rates, wet_blocks, surface_light):
    return pl.pallas_call(
        finish_kernel,
        out_shape=(f32(4, LANES, LANES), bf16(TRACERS, LANES, LANES), f32(LANES, LANES)),
        in_specs=smem(1) + vmem(6) + hbm(3),
        out_specs=hbm(3),
        scratch_shapes=STEP_SCRATCH
        + [
            pltpu.VMEM((len(SPEEDS), LEVELS, LANES), jnp.float32),
            pltpu.VMEM((2 * LANES, LANES), jnp.float32),
            pltpu.VMEM((2, 12, LEVELS, LANES), jnp.float32),
            pltpu.VMEM((2, ROWS, LEVELS, LANES), jnp.float32),
            pltpu.VMEM((4, ROWS, LEVELS, LANES), jnp.float32),
            pltpu.VMEM((TRACERS, LANES, LANES), jnp.float32),
            pltpu.VMEM((TRACERS, LANES, LANES), jnp.bfloat16),
            pltpu.VMEM((4, LANES, LANES), jnp.float32),
            pltpu.VMEM((LANES, LANES), jnp.float32),
            pltpu.SMEM(rates.shape, jnp.float32),
            pltpu.SMEM(wet_blocks.shape, jnp.int32),
            pltpu.VMEM(surface_light.shape, jnp.float32),
            pltpu.SemaphoreType.DMA((3 + 3 * BLOCKS,)),
        ],
        compiler_params=limit(12),
        name="finish",
    )(flags, *main, *halos, *map(in_hbm, (rates, wet_blocks, surface_light)))


def shards(ocean, tracers, wet_blocks, surface_light, rates):
    tr = tracers.reshape(TRACERS, LANES, LANES)
    oc = ocean.reshape(4, LANES, LANES)
    groups, tiles = lax.axis_size("grp"), lax.axis_size("tile")

    def ahead(x, axis, count):
        return lax.ppermute(x, axis, [(i, i + 1) for i in range(count - 1)])

    def back(x, axis, count):
        return lax.ppermute(x, axis, [(i + 1, i) for i in range(count - 1)])

    within = [(i, i ^ 1) for i in range(groups) if i ^ 1 < groups]
    between = [pair for i in range(1, groups - 1, 2) for pair in ((i, i + 1), (i + 1, i))]
    g, t = lax.axis_index("grp"), lax.axis_index("tile")
    flags = jnp.stack([g > 0, g < groups - 1, t > 0, t < tiles - 1, g % 2 == 0]).astype(jnp.float32)
    mine, own_ocean, edges = pack(tr, oc)
    edges_far = lax.ppermute(edges, "grp", between)
    edges_near = lax.ppermute(edges, "grp", within)
    far = lax.ppermute(mine, "grp", between)
    near = lax.ppermute(mine, "grp", within)
    even, half = g % 2 == 0, 2 * LEVELS
    edges_before = jnp.where(even, edges_far[half:], edges_near[half:])
    edges_after = jnp.where(even, edges_near[:half], edges_far[:half])
    edges = jnp.concatenate([edges_before, edges, edges_after], axis=0)
    from_left = ahead(edges, "tile", tiles)
    from_right = back(edges, "tile", tiles)
    main = transport(flags, mine, near, far, own_ocean)
    ocean_out, tracer_out, heating = finish(
        flags, main, (from_left, from_right), rates, wet_blocks, surface_light
    )
    return (
        ocean_out.reshape(ocean.shape),
        tracer_out.reshape(tracers.shape),
        heating.reshape(LEVELS, ROWS, LANES),
    )


def solution(mesh):
    return jax.shard_map(
        shards,
        mesh=mesh,
        in_specs=(
            P(None, None, "grp", "tile"),
            P(None, None, "grp", "tile"),
            P("grp", "tile"),
            P("grp", "tile"),
            P(),
        ),
        out_specs=(
            P(None, None, "grp", "tile"),
            P(None, None, "grp", "tile"),
            P(None, "grp", "tile"),
        ),
        check_vma=False,
    )
```
